256 devices in a mesh: space: 32 (over z_hi, x, core), tm: 8 (over z_lo, y).
Axes of the slice: x: 4, y: 4, z: 8 (z_hi: 4, z_lo: 2; z = z_hi * 2 + z_lo), core: 2. Of those that a mesh axis runs over, the one named last changes fastest.
Arguments:
- start_state: float32 [1024, 8192], P('space'), may hold values from -6 to 6
- old_starts: float32 [8, 1024, 8192], P('tm', 'space'), may hold values from -6 to 6
- conductivity: float32 [1024, 8192], P('space'), may hold values from 0.1 to 0.7
- velocity: float32 [2, 1024, 8192], P(None, 'space'), may hold values from -0.2 to 0.2
- coarse_gain: float32 [8, 1024, 8192], P('tm', 'space'), may hold values from 0.4 to 0.99
- targets: float32 [8, 1024, 8192], P('tm', 'space'), may hold values from -6 to 6
Outputs:
- new_ends: float32 [8, 1024, 8192], P('tm', 'space')
- gradient: float32 [1024, 8192], P('space')
The draws below stay inside these ranges and needn't reach their ends.
All inputs are finite; a program needn't handle non-finite values.
Results may differ from the reference program's by a relative error of at most 0.00002.
Values sent between devices are 32-bit elements; how exact they have to be, the bound alone decides.
A program may use at most 128 MiB of HBM per device.

```python
import math
import jax
import jax.numpy as jnp
from jax import lax

COLS = 8192
STEPS = 4
SLABS = 8
NX = 1024


def block_levels(key, extent, pieces, smallest, high):
    def one(axis_at, shards_of):
        draws = jax.random.uniform(jax.random.fold_in(jax.random.fold_in(key, 6), axis_at), (shards_of,), jnp.float32, smallest / len(pieces), high / len(pieces))
        return jnp.repeat(jnp.exp(draws), extent[axis_at] // shards_of).reshape((-1,) + (1,) * (len(extent) - axis_at - 1))

    level = one(*pieces[0])
    for cut in pieces[1:]:
        level = level * one(*cut)
    return level


def bell_draw(own_key, dims, scale, reach, pieces=(), kind=jnp.bfloat16):
    level = block_levels(own_key, dims, pieces, -0.22, 0.18) if pieces else 1.0
    array = jax.random.normal(own_key, dims, jnp.float32) * scale * level
    return jnp.minimum(jnp.maximum(array, -reach), reach).astype(kind)


def setup_inputs(seed: int = 0) -> dict:
    streams_of = jax.random.split(jax.random.key(seed), 7)
    start_state = bell_draw(streams_of[0], (NX, COLS), 1.0, 6.0, ((0, 32),), jnp.float32)
    old_starts = bell_draw(streams_of[1], (SLABS, NX, COLS), 1.0, 6.0, ((0, 8), (1, 32)), jnp.float32)
    conductivity = jnp.clip(jnp.exp(math.log(0.7) - 1.9459101 * jax.random.uniform(streams_of[2], (NX, COLS), jnp.float32) ** block_levels(streams_of[2], (NX, COLS), ((0, 32),), -0.2, 0.2)), 0.1, 0.7)
    velocity = jnp.clip(jax.random.uniform(streams_of[3], (2, NX, COLS), jnp.float32, -0.2, 0.2) * block_levels(streams_of[3], (2, NX, COLS), ((1, 32),), -0.4, 0.0), -0.2, 0.2)
    coarse_gain = jnp.clip(jnp.exp(math.log(0.99) - 0.9062404 * jax.random.uniform(streams_of[4], (SLABS, NX, COLS), jnp.float32) ** block_levels(streams_of[4], (SLABS, NX, COLS), ((0, 8), (1, 32)), -0.2, 0.2)), 0.4, 0.99)
    targets = bell_draw(streams_of[5], (SLABS, NX, COLS), 1.0, 6.0, ((0, 8), (1, 32)), jnp.float32)
    return dict(start_state=start_state, old_starts=old_starts, conductivity=conductivity, velocity=velocity, coarse_gain=coarse_gain, targets=targets)


time_step = 0.25

def potential(field):
    return field + 0.25 * jnp.tanh(field)

def advance(padded, kappa, velocity):
    wide = jnp.pad(padded, ((0, 0), (1, 1)))
    shaped = potential(wide)
    centre = wide[1:-1, 1:-1]
    spread = shaped[:-2, 1:-1] + shaped[2:, 1:-1] + shaped[1:-1, :-2] + shaped[1:-1, 2:] - 4.0 * shaped[1:-1, 1:-1]
    along_rows = velocity[0]
    along_cols = velocity[1]
    transport = jnp.maximum(along_rows, 0.0) * (centre - wide[:-2, 1:-1]) + jnp.minimum(along_rows, 0.0) * (wide[2:, 1:-1] - centre) + jnp.maximum(along_cols, 0.0) * (centre - wide[1:-1, :-2]) + jnp.minimum(along_cols, 0.0) * (wide[1:-1, 2:] - centre)
    return centre + time_step * (kappa * spread - transport)

def fine(begin, kappa, velocity):
    field = begin
    for step in range(STEPS):
        field = advance(jnp.pad(field, ((1, 1), (0, 0))), kappa, velocity)
    return field

def reference(start_state, old_starts, conductivity, velocity, coarse_gain, targets):
    count = old_starts.shape[0]
    fine_ends = lax.map(lambda begin: fine(begin, conductivity, velocity), old_starts)
    carried = fine_ends - coarse_gain * old_starts
    ends = []
    begin = start_state
    for slab in range(count):
        finish = coarse_gain[slab] * begin + carried[slab]
        ends.append(finish)
        begin = finish
    new_ends = jnp.stack(ends)
    misfit = new_ends - targets
    adjoints = [misfit[count - 1]]
    for slab in range(count - 2, -1, -1):
        adjoints.insert(0, misfit[slab] + coarse_gain[slab + 1] * adjoints[0])
    adjoint_stack = jnp.stack(adjoints)

    def accumulate(total, pair):
        begin_here, weight = pair
        unused, pullback = jax.vjp(lambda kappa: fine(begin_here, kappa, velocity), conductivity)
        return (total + pullback(weight)[0], None)
    gradient, unused = lax.scan(accumulate, jnp.zeros_like(conductivity), (old_starts, adjoint_stack))
    return (new_ends, gradient)
```

```python
import jax
import jax.numpy as jnp
from jax import lax
from jax.sharding import PartitionSpec as P

STEPS = 4
HALO = 8


time_step = 0.25


def with_halo(cells, axis, dim):
    count = lax.axis_size(axis)
    ends = count - 1
    head = lax.slice_in_dim(cells, 0, 1, axis=dim)
    tail = lax.slice_in_dim(cells, cells.shape[dim] - 1, cells.shape[dim], axis=dim)
    return jnp.concatenate(
        [
            lax.ppermute(tail, axis, [(i, (i + 1) % count) for i in range(ends)]),
            cells,
            lax.ppermute(head, axis, [((i + 1) % count, i) for i in range(ends)]),
        ],
        axis=dim,
    )


def potential(field):
    return field + 0.25 * jnp.tanh(field)


def advance(padded, kappa, along_rows, along_cols):
    wide = jnp.pad(padded, ((0, 0), (0, 0), (1, 1)))
    shaped = potential(wide)
    centre = wide[:, 1:-1, 1:-1]
    spread = (
        shaped[:, :-2, 1:-1]
        + shaped[:, 2:, 1:-1]
        + shaped[:, 1:-1, :-2]
        + shaped[:, 1:-1, 2:]
        - 4.0 * shaped[:, 1:-1, 1:-1]
    )
    transport = (
        jnp.maximum(along_rows, 0.0) * (centre - wide[:, :-2, 1:-1])
        + jnp.minimum(along_rows, 0.0) * (wide[:, 2:, 1:-1] - centre)
        + jnp.maximum(along_cols, 0.0) * (centre - wide[:, 1:-1, :-2])
        + jnp.minimum(along_cols, 0.0) * (wide[:, 1:-1, 2:] - centre)
    )
    return centre + time_step * (kappa * spread - transport)


def fine(field, kappa, along_rows, along_cols, inside):
    for step in range(STEPS):
        padded = with_halo(field, "space", 1)
        field = jnp.where(inside, advance(padded, kappa, along_rows, along_cols), 0.0)
    return field


def pad_cols(x):
    return jnp.pad(x, [(0, 0)] * (x.ndim - 1) + [(HALO, HALO)])


def own_window(x, start, width):
    return lax.dynamic_slice_in_dim(pad_cols(x), start, width, axis=x.ndim - 1)


def on_device(start_state, old_starts, conductivity, velocity, coarse_gain, targets):
    blocks = lax.axis_size("tm")
    block = lax.axis_index("tm")
    rows, cols = start_state.shape
    width = cols // blocks
    wide = width + 2 * HALO

    def send_windows(x):
        padded = pad_cols(x)
        return jnp.stack([padded[:, k * width : k * width + wide] for k in range(blocks)])

    def to_blocks(x):
        return lax.all_to_all(send_windows(x), "tm", 0, 0, tiled=True)

    old = to_blocks(old_starts[0])
    gain = to_blocks(coarse_gain[0])
    target = to_blocks(targets[0])

    first = block * width
    kappa = own_window(conductivity, first, wide)
    flow = own_window(velocity, first, wide)
    begin = own_window(start_state, first, wide)
    column = first - HALO + lax.broadcasted_iota(jnp.int32, (1, 1, wide), 2)
    inside = (column >= 0) & (column < cols)

    fine_ends, pullback = jax.vjp(
        lambda k: fine(old, k, flow[0], flow[1], inside), kappa
    )
    carried = fine_ends - gain * old
    ends = []
    for slab in range(blocks):
        begin = gain[slab] * begin + carried[slab]
        ends.append(begin)
    new_ends = jnp.stack(ends)
    misfit = new_ends - target
    adjoints = [misfit[blocks - 1]]
    for slab in range(blocks - 2, -1, -1):
        adjoints.insert(0, misfit[slab] + gain[slab + 1] * adjoints[0])
    adjoint = jnp.stack(adjoints)
    (grad_window,) = pullback(adjoint)

    interior = new_ends[:, :, HALO : HALO + width]
    new_end = lax.all_to_all(interior, "tm", 0, 2, tiled=True)
    gradient = lax.all_gather(grad_window[:, HALO : HALO + width], "tm", axis=1, tiled=True)
    return (new_end, gradient)


def solution(mesh):
    in_specs = (
        P("space", None),
        P("tm", "space", None),
        P("space", None),
        P(None, "space", None),
        P("tm", "space", None),
        P("tm", "space", None),
    )
    out_specs = (P("tm", "space", None), P("space", None))
    return jax.shard_map(
        on_device, mesh=mesh, in_specs=in_specs, out_specs=out_specs, check_vma=False
    )
```

```python
import jax
import jax.numpy as jnp
from jax import lax
from jax.sharding import PartitionSpec as P

STEPS = 4
HALO = 8


time_step = 0.25


def with_halo(cells, axis, dim, width):
    count = lax.axis_size(axis)
    ends = count - 1
    head = lax.slice_in_dim(cells, 0, width, axis=dim)
    tail = lax.slice_in_dim(cells, cells.shape[dim] - width, cells.shape[dim], axis=dim)
    return jnp.concatenate(
        [
            lax.ppermute(tail, axis, [(i, (i + 1) % count) for i in range(ends)]),
            cells,
            lax.ppermute(head, axis, [((i + 1) % count, i) for i in range(ends)]),
        ],
        axis=dim,
    )


def potential(field):
    return field + 0.25 * jnp.tanh(field)


def advance(field, kappa, along_rows, along_cols):
    wide = jnp.pad(field, ((0, 0), (1, 1), (1, 1)))
    shaped = potential(wide)
    centre = wide[:, 1:-1, 1:-1]
    spread = (
        shaped[:, :-2, 1:-1]
        + shaped[:, 2:, 1:-1]
        + shaped[:, 1:-1, :-2]
        + shaped[:, 1:-1, 2:]
        - 4.0 * shaped[:, 1:-1, 1:-1]
    )
    transport = (
        jnp.maximum(along_rows, 0.0) * (centre - wide[:, :-2, 1:-1])
        + jnp.minimum(along_rows, 0.0) * (wide[:, 2:, 1:-1] - centre)
        + jnp.maximum(along_cols, 0.0) * (centre - wide[:, 1:-1, :-2])
        + jnp.minimum(along_cols, 0.0) * (wide[:, 1:-1, 2:] - centre)
    )
    return centre + time_step * (kappa * spread - transport)


def fine(field, kappa, along_rows, along_cols, inside):
    kappa = with_halo(kappa, "space", 0, STEPS)
    for step in range(STEPS):
        field = jnp.where(inside, advance(field, kappa, along_rows, along_cols), 0.0)
    return field[:, STEPS:-STEPS]


def pad_cols(x):
    return jnp.pad(x, [(0, 0)] * (x.ndim - 1) + [(HALO, HALO)])


def own_window(x, start, width):
    return lax.dynamic_slice_in_dim(pad_cols(x), start, width, axis=x.ndim - 1)


def on_device(start_state, old_starts, conductivity, velocity, coarse_gain, targets):
    blocks = lax.axis_size("tm")
    block = lax.axis_index("tm")
    rows, cols = start_state.shape
    width = cols // blocks
    wide = width + 2 * HALO

    def send_windows(x):
        padded = pad_cols(x)
        return jnp.stack([padded[:, k * width : k * width + wide] for k in range(blocks)])

    def to_blocks(x):
        return lax.all_to_all(send_windows(x), "tm", 0, 0, tiled=True)

    old = to_blocks(old_starts[0])
    gain = to_blocks(coarse_gain[0])
    target = to_blocks(targets[0])

    first = block * width
    kappa = own_window(conductivity, first, wide)
    flow = own_window(velocity, first, wide)
    begin = own_window(start_state, first, wide)
    column = first - HALO + lax.broadcasted_iota(jnp.int32, (1, 1, wide), 2)
    strip = lax.axis_index("space")
    row = strip * rows - STEPS + lax.broadcasted_iota(jnp.int32, (1, rows + 2 * STEPS, 1), 1)
    inside = (column >= 0) & (column < cols) & (row >= 0) & (row < rows * lax.axis_size("space"))
    old_rows = with_halo(old, "space", 1, STEPS)
    flow_rows = with_halo(flow, "space", 1, STEPS)

    fine_ends, pullback = jax.vjp(
        lambda k: fine(old_rows, k, flow_rows[0], flow_rows[1], inside), kappa
    )
    carried = fine_ends - gain * old
    ends = []
    for slab in range(blocks):
        begin = gain[slab] * begin + carried[slab]
        ends.append(begin)
    new_ends = jnp.stack(ends)
    misfit = new_ends - target
    adjoints = [misfit[blocks - 1]]
    for slab in range(blocks - 2, -1, -1):
        adjoints.insert(0, misfit[slab] + gain[slab + 1] * adjoints[0])
    adjoint = jnp.stack(adjoints)
    (grad_window,) = pullback(adjoint)

    interior = new_ends[:, :, HALO : HALO + width]
    new_end = lax.all_to_all(interior, "tm", 0, 2, tiled=True)
    own = grad_window[:, HALO : HALO + width]
    copies = jnp.broadcast_to(own[None], (blocks,) + own.shape)
    gradient = lax.all_to_all(copies, "tm", 0, 2, tiled=True)[0]
    return (new_end, gradient)


def solution(mesh):
    in_specs = (
        P("space", None),
        P("tm", "space", None),
        P("space", None),
        P(None, "space", None),
        P("tm", "space", None),
        P("tm", "space", None),
    )
    out_specs = (P("tm", "space", None), P("space", None))
    return jax.shard_map(
        on_device, mesh=mesh, in_specs=in_specs, out_specs=out_specs, check_vma=False
    )
```

```python
import jax
import jax.numpy as jnp
from jax import lax
from jax.experimental import pallas as pl
from jax.sharding import PartitionSpec as P

STEPS = 4
HALO = 8


time_step = 0.25


def with_halo(cells, axis, dim, width):
    count = lax.axis_size(axis)
    ends = count - 1
    head = lax.slice_in_dim(cells, 0, width, axis=dim)
    tail = lax.slice_in_dim(cells, cells.shape[dim] - width, cells.shape[dim], axis=dim)
    return jnp.concatenate(
        [
            lax.ppermute(tail, axis, [(i, (i + 1) % count) for i in range(ends)]),
            cells,
            lax.ppermute(head, axis, [((i + 1) % count, i) for i in range(ends)]),
        ],
        axis=dim,
    )


def potential(field):
    return field + 0.25 * jnp.tanh(field)


def advance(field, kappa, along_rows, along_cols):
    wide = jnp.pad(field, ((0, 0), (1, 1), (1, 1)))
    shaped = potential(wide)
    centre = wide[:, 1:-1, 1:-1]
    spread = (
        shaped[:, :-2, 1:-1]
        + shaped[:, 2:, 1:-1]
        + shaped[:, 1:-1, :-2]
        + shaped[:, 1:-1, 2:]
        - 4.0 * shaped[:, 1:-1, 1:-1]
    )
    transport = (
        jnp.maximum(along_rows, 0.0) * (centre - wide[:, :-2, 1:-1])
        + jnp.minimum(along_rows, 0.0) * (wide[:, 2:, 1:-1] - centre)
        + jnp.maximum(along_cols, 0.0) * (centre - wide[:, 1:-1, :-2])
        + jnp.minimum(along_cols, 0.0) * (wide[:, 1:-1, 2:] - centre)
    )
    return centre + time_step * (kappa * spread - transport)


def fine(field, kappa, along_rows, along_cols, inside):
    kappa = with_halo(kappa, "space", 0, STEPS)
    for step in range(STEPS):
        field = jnp.where(inside, advance(field, kappa, along_rows, along_cols), 0.0)
    return field[:, STEPS:-STEPS]


def pad_cols(x):
    return jnp.pad(x, [(0, 0)] * (x.ndim - 1) + [(HALO, HALO)])


def own_window(x, start, width):
    return lax.dynamic_slice_in_dim(pad_cols(x), start, width, axis=x.ndim - 1)


def scan_kernel(fine_ref, old_ref, gain_ref, target_ref, begin_ref, ends_ref, adjoint_ref):
    slabs = fine_ref.shape[0]
    begin = begin_ref[...]
    for slab in range(slabs):
        carried = fine_ref[slab] - gain_ref[slab] * old_ref[slab]
        begin = gain_ref[slab] * begin + carried
        ends_ref[slab] = begin
    adjoint = ends_ref[slabs - 1] - target_ref[slabs - 1]
    adjoint_ref[slabs - 1] = adjoint
    for slab in range(slabs - 2, -1, -1):
        adjoint = (ends_ref[slab] - target_ref[slab]) + gain_ref[slab + 1] * adjoint
        adjoint_ref[slab] = adjoint


def scans(fine_ends, old, gain, target, begin):
    slabs, rows, wide = fine_ends.shape
    tile = 8
    stacked = pl.BlockSpec((slabs, tile, wide), lambda i: (0, i, 0))
    single = pl.BlockSpec((tile, wide), lambda i: (i, 0))
    shape = jax.ShapeDtypeStruct(fine_ends.shape, fine_ends.dtype)
    return pl.pallas_call(
        scan_kernel,
        grid=(rows // tile,),
        in_specs=[stacked, stacked, stacked, stacked, single],
        out_specs=[stacked, stacked],
        out_shape=[shape, shape],
    )(fine_ends, old, gain, target, begin)


def on_device(start_state, old_starts, conductivity, velocity, coarse_gain, targets):
    blocks = lax.axis_size("tm")
    block = lax.axis_index("tm")
    rows, cols = start_state.shape
    width = cols // blocks
    wide = width + 2 * HALO

    def send_windows(x):
        main = x.reshape(rows, blocks, width).transpose(1, 0, 2)
        left = jnp.pad(main[:-1, :, width - HALO :], ((1, 0), (0, 0), (0, 0)))
        right = jnp.pad(main[1:, :, :HALO], ((0, 1), (0, 0), (0, 0)))
        return jnp.concatenate([left, main, right], axis=2)

    def to_blocks(x):
        return lax.all_to_all(send_windows(x), "tm", 0, 0, tiled=True)

    old = to_blocks(old_starts[0])
    gain = to_blocks(coarse_gain[0])
    target = to_blocks(targets[0])

    first = block * width
    kappa = own_window(conductivity, first, wide)
    flow = own_window(velocity, first, wide)
    begin = own_window(start_state, first, wide)
    column = first - HALO + lax.broadcasted_iota(jnp.int32, (1, 1, wide), 2)
    strip = lax.axis_index("space")
    row = strip * rows - STEPS + lax.broadcasted_iota(jnp.int32, (1, rows + 2 * STEPS, 1), 1)
    inside = (column >= 0) & (column < cols) & (row >= 0) & (row < rows * lax.axis_size("space"))
    old_rows = with_halo(old, "space", 1, STEPS)
    flow_rows = with_halo(flow, "space", 1, STEPS)

    fine_ends, pullback = jax.vjp(
        lambda k: fine(old_rows, k, flow_rows[0], flow_rows[1], inside), kappa
    )
    new_ends, adjoint = scans(fine_ends, old, gain, target, begin)
    (grad_window,) = pullback(adjoint)

    interior = new_ends[:, :, HALO : HALO + width]
    new_end = lax.all_to_all(interior, "tm", 0, 2, tiled=True)
    own = grad_window[:, HALO : HALO + width]
    copies = jnp.broadcast_to(own[None], (blocks,) + own.shape)
    gradient = lax.all_to_all(copies, "tm", 0, 2, tiled=True)[0]
    return (new_end, gradient)


def solution(mesh):
    in_specs = (
        P("space", None),
        P("tm", "space", None),
        P("space", None),
        P(None, "space", None),
        P("tm", "space", None),
        P("tm", "space", None),
    )
    out_specs = (P("tm", "space", None), P("space", None))
    return jax.shard_map(
        on_device, mesh=mesh, in_specs=in_specs, out_specs=out_specs, check_vma=False
    )
```

```python
import jax
import jax.numpy as jnp
from jax import lax
from jax.experimental import pallas as pl
from jax.sharding import PartitionSpec as P

STEPS = 4
HALO = 8


time_step = 0.25


def with_halo(cells, axis, dim, width):
    count = lax.axis_size(axis)
    ends = count - 1
    head = lax.slice_in_dim(cells, 0, width, axis=dim)
    tail = lax.slice_in_dim(cells, cells.shape[dim] - width, cells.shape[dim], axis=dim)
    return jnp.concatenate(
        [
            lax.ppermute(tail, axis, [(i, (i + 1) % count) for i in range(ends)]),
            cells,
            lax.ppermute(head, axis, [((i + 1) % count, i) for i in range(ends)]),
        ],
        axis=dim,
    )


def potential(field):
    return field + 0.25 * jnp.tanh(field)


def advance(field, kappa, along_rows, along_cols):
    wide = jnp.pad(field, ((0, 0), (1, 1), (1, 1)))
    shaped = potential(wide)
    centre = wide[:, 1:-1, 1:-1]
    spread = (
        shaped[:, :-2, 1:-1]
        + shaped[:, 2:, 1:-1]
        + shaped[:, 1:-1, :-2]
        + shaped[:, 1:-1, 2:]
        - 4.0 * shaped[:, 1:-1, 1:-1]
    )
    transport = (
        jnp.maximum(along_rows, 0.0) * (centre - wide[:, :-2, 1:-1])
        + jnp.minimum(along_rows, 0.0) * (wide[:, 2:, 1:-1] - centre)
        + jnp.maximum(along_cols, 0.0) * (centre - wide[:, 1:-1, :-2])
        + jnp.minimum(along_cols, 0.0) * (wide[:, 1:-1, 2:] - centre)
    )
    return centre + time_step * (kappa * spread - transport)


def fine(field, kappa, along_rows, along_cols, inside):
    kappa = with_halo(kappa, "space", 0, STEPS)
    for step in range(STEPS):
        field = jnp.where(inside, advance(field, kappa, along_rows, along_cols), 0.0)
    return field[:, STEPS:-STEPS]


def pad_cols(x):
    return jnp.pad(x, [(0, 0)] * (x.ndim - 1) + [(HALO, HALO)])


def own_window(x, start, width):
    return lax.dynamic_slice_in_dim(pad_cols(x), start, width, axis=x.ndim - 1)


def scan_kernel(fine_ref, old_ref, gain_ref, target_ref, begin_ref, ends_ref, adjoint_ref):
    slabs = fine_ref.shape[0]
    begin = begin_ref[...]
    for slab in range(slabs):
        carried = fine_ref[slab] - gain_ref[slab] * old_ref[slab]
        begin = gain_ref[slab] * begin + carried
        ends_ref[slab] = begin
    adjoint = ends_ref[slabs - 1] - target_ref[slabs - 1]
    adjoint_ref[slabs - 1] = adjoint
    for slab in range(slabs - 2, -1, -1):
        adjoint = (ends_ref[slab] - target_ref[slab]) + gain_ref[slab + 1] * adjoint
        adjoint_ref[slab] = adjoint


def scans(fine_ends, old, gain, target, begin):
    slabs, rows, wide = fine_ends.shape
    tile = 8
    stacked = pl.BlockSpec((slabs, tile, wide), lambda i: (0, i, 0))
    single = pl.BlockSpec((tile, wide), lambda i: (i, 0))
    shape = jax.ShapeDtypeStruct(fine_ends.shape, fine_ends.dtype)
    return pl.pallas_call(
        scan_kernel,
        grid=(rows // tile,),
        in_specs=[stacked, stacked, stacked, stacked, single],
        out_specs=[stacked, stacked],
        out_shape=[shape, shape],
    )(fine_ends, old, gain, target, begin)


def on_device(start_state, old_starts, conductivity, velocity, coarse_gain, targets):
    blocks = lax.axis_size("tm")
    block = lax.axis_index("tm")
    rows, cols = start_state.shape
    width = cols // blocks
    wide = width + 2 * HALO

    def send_windows(x):
        main = x.reshape(rows, blocks, width).transpose(1, 0, 2)
        left = jnp.pad(main[:-1, :, width - HALO :], ((1, 0), (0, 0), (0, 0)))
        right = jnp.pad(main[1:, :, :HALO], ((0, 1), (0, 0), (0, 0)))
        return jnp.concatenate([left, main, right], axis=2)

    def to_blocks(x):
        return lax.all_to_all(send_windows(x), "tm", 0, 0, tiled=True)

    old = to_blocks(old_starts[0])
    pair = lax.all_to_all(
        jnp.stack([send_windows(coarse_gain[0]), send_windows(targets[0])], axis=1),
        "tm", 0, 0, tiled=True,
    )
    gain = pair[:, 0]
    target = pair[:, 1]
    old, conductivity, velocity, start_state = lax.optimization_barrier(
        (old, conductivity, velocity, start_state)
    )

    first = block * width
    kappa = own_window(conductivity, first, wide)
    flow = own_window(velocity, first, wide)
    begin = own_window(start_state, first, wide)
    column = first - HALO + lax.broadcasted_iota(jnp.int32, (1, 1, wide), 2)
    strip = lax.axis_index("space")
    row = strip * rows - STEPS + lax.broadcasted_iota(jnp.int32, (1, rows + 2 * STEPS, 1), 1)
    inside = (column >= 0) & (column < cols) & (row >= 0) & (row < rows * lax.axis_size("space"))
    old_rows = with_halo(old, "space", 1, STEPS)
    flow_rows = with_halo(flow, "space", 1, STEPS)

    fine_ends, pullback = jax.vjp(
        lambda k: fine(old_rows, k, flow_rows[0], flow_rows[1], inside), kappa
    )
    new_ends, adjoint = scans(fine_ends, old, gain, target, begin)
    (grad_window,) = pullback(adjoint)

    interior = new_ends[:, :, HALO : HALO + width]
    new_end = lax.all_to_all(interior, "tm", 0, 2, tiled=True)
    own = grad_window[:, HALO : HALO + width]
    copies = jnp.broadcast_to(own[None], (blocks,) + own.shape)
    gradient = lax.all_to_all(copies, "tm", 0, 2, tiled=True)[0]
    return (new_end, gradient)


def solution(mesh):
    in_specs = (
        P("space", None),
        P("tm", "space", None),
        P("space", None),
        P(None, "space", None),
        P("tm", "space", None),
        P("tm", "space", None),
    )
    out_specs = (P("tm", "space", None), P("space", None))
    return jax.shard_map(
        on_device, mesh=mesh, in_specs=in_specs, out_specs=out_specs, check_vma=False
    )
```

```python
import jax
import jax.numpy as jnp
from jax import lax
from jax.experimental import pallas as pl
from jax.sharding import PartitionSpec as P

STEPS = 4
HALO = 8


time_step = 0.25


def with_halo(cells, axis, dim, width):
    count = lax.axis_size(axis)
    ends = count - 1
    head = lax.slice_in_dim(cells, 0, width, axis=dim)
    tail = lax.slice_in_dim(cells, cells.shape[dim] - width, cells.shape[dim], axis=dim)
    return jnp.concatenate(
        [
            lax.ppermute(tail, axis, [(i, (i + 1) % count) for i in range(ends)]),
            cells,
            lax.ppermute(head, axis, [((i + 1) % count, i) for i in range(ends)]),
        ],
        axis=dim,
    )


def potential(field):
    return field + 0.25 * jnp.tanh(field)


def advance(field, kappa, along_rows, along_cols):
    wide = jnp.pad(field, ((0, 0), (1, 1), (1, 1)))
    shaped = potential(wide)
    centre = wide[:, 1:-1, 1:-1]
    spread = (
        shaped[:, :-2, 1:-1]
        + shaped[:, 2:, 1:-1]
        + shaped[:, 1:-1, :-2]
        + shaped[:, 1:-1, 2:]
        - 4.0 * shaped[:, 1:-1, 1:-1]
    )
    transport = (
        jnp.maximum(along_rows, 0.0) * (centre - wide[:, :-2, 1:-1])
        + jnp.minimum(along_rows, 0.0) * (wide[:, 2:, 1:-1] - centre)
        + jnp.maximum(along_cols, 0.0) * (centre - wide[:, 1:-1, :-2])
        + jnp.minimum(along_cols, 0.0) * (wide[:, 1:-1, 2:] - centre)
    )
    return centre + time_step * (kappa * spread - transport)


def fine(field, kappa, along_rows, along_cols, inside):
    for step in range(STEPS):
        field = jnp.where(inside, advance(field, kappa, along_rows, along_cols), 0.0)
    return field[:, STEPS:-STEPS]


def pad_cols(x):
    return jnp.pad(x, [(0, 0)] * (x.ndim - 1) + [(HALO, HALO)])


def own_window(x, start, width):
    return lax.dynamic_slice_in_dim(pad_cols(x), start, width, axis=x.ndim - 1)


def scan_kernel(fine_ref, old_ref, pair_ref, begin_ref, ends_ref, adjoint_ref):
    slabs = fine_ref.shape[0]
    begin = begin_ref[...]
    for slab in range(slabs):
        carried = fine_ref[slab] - pair_ref[slab, 0] * old_ref[slab]
        begin = pair_ref[slab, 0] * begin + carried
        ends_ref[slab] = begin
    adjoint = ends_ref[slabs - 1] - pair_ref[slabs - 1, 1]
    adjoint_ref[slabs - 1] = adjoint
    for slab in range(slabs - 2, -1, -1):
        adjoint = (ends_ref[slab] - pair_ref[slab, 1]) + pair_ref[slab + 1, 0] * adjoint
        adjoint_ref[slab] = adjoint


def scans(fine_ends, old, pair, begin):
    slabs, rows, wide = fine_ends.shape
    tile = 8
    stacked = pl.BlockSpec((slabs, tile, wide), lambda i: (0, i, 0))
    both = pl.BlockSpec((slabs, 2, tile, wide), lambda i: (0, 0, i, 0))
    single = pl.BlockSpec((tile, wide), lambda i: (i, 0))
    shape = jax.ShapeDtypeStruct(fine_ends.shape, fine_ends.dtype)
    return pl.pallas_call(
        scan_kernel,
        grid=(rows // tile,),
        in_specs=[stacked, stacked, both, single],
        out_specs=[stacked, stacked],
        out_shape=[shape, shape],
    )(fine_ends, old, pair, begin)


def on_device(start_state, old_starts, conductivity, velocity, coarse_gain, targets):
    blocks = lax.axis_size("tm")
    block = lax.axis_index("tm")
    rows, cols = start_state.shape
    width = cols // blocks
    wide = width + 2 * HALO

    def send_windows(x):
        main = x.reshape(rows, blocks, width).transpose(1, 0, 2)
        left = jnp.pad(main[:-1, :, width - HALO :], ((1, 0), (0, 0), (0, 0)))
        right = jnp.pad(main[1:, :, :HALO], ((0, 1), (0, 0), (0, 0)))
        return jnp.concatenate([left, main, right], axis=2)

    def to_blocks(x):
        return lax.all_to_all(send_windows(x), "tm", 0, 0, tiled=True)

    old = to_blocks(old_starts[0])
    pair = lax.all_to_all(
        jnp.stack([send_windows(coarse_gain[0]), send_windows(targets[0])], axis=1),
        "tm", 0, 0, tiled=True,
    )
    old, conductivity, velocity, start_state = lax.optimization_barrier(
        (old, conductivity, velocity, start_state)
    )

    first = block * width
    kappa = own_window(conductivity, first, wide)
    flow = own_window(velocity, first, wide)
    begin = own_window(start_state, first, wide)
    column = first - HALO + lax.broadcasted_iota(jnp.int32, (1, 1, wide), 2)
    strip = lax.axis_index("space")
    row = strip * rows - STEPS + lax.broadcasted_iota(jnp.int32, (1, rows + 2 * STEPS, 1), 1)
    inside = (column >= 0) & (column < cols) & (row >= 0) & (row < rows * lax.axis_size("space"))
    slabs = old.shape[0]
    fields = jnp.concatenate([old, kappa[None], flow], axis=0)
    fields = with_halo(fields, "space", 1, STEPS)
    old_rows = fields[:slabs]
    kappa_rows = fields[slabs]
    flow_rows = fields[slabs + 1 :]

    fine_ends, pullback = jax.vjp(
        lambda k: fine(old_rows, k, flow_rows[0], flow_rows[1], inside), kappa_rows
    )
    new_ends, adjoint = scans(fine_ends, old, pair, begin)
    (grad_rows,) = pullback(adjoint)
    count = lax.axis_size("space")
    ends = count - 1
    from_below = lax.ppermute(grad_rows[:STEPS], "space", [((i + 1) % count, i) for i in range(ends)])
    from_above = lax.ppermute(grad_rows[-STEPS:], "space", [(i, (i + 1) % count) for i in range(ends)])
    grad_window = grad_rows[STEPS:-STEPS]
    grad_window = grad_window.at[-STEPS:].add(from_below).at[:STEPS].add(from_above)

    interior = new_ends[:, :, HALO : HALO + width]
    new_end = lax.all_to_all(interior, "tm", 0, 2, tiled=True)
    own = grad_window[:, HALO : HALO + width]
    copies = jnp.broadcast_to(own[None], (blocks,) + own.shape)
    gradient = lax.all_to_all(copies, "tm", 0, 2, tiled=True)[0]
    return (new_end, gradient)


def solution(mesh):
    in_specs = (
        P("space", None),
        P("tm", "space", None),
        P("space", None),
        P(None, "space", None),
        P("tm", "space", None),
        P("tm", "space", None),
    )
    out_specs = (P("tm", "space", None), P("space", None))
    return jax.shard_map(
        on_device, mesh=mesh, in_specs=in_specs, out_specs=out_specs, check_vma=False
    )
```

```python
import jax
import jax.numpy as jnp
from jax import lax
from jax.experimental import pallas as pl
from jax.sharding import PartitionSpec as P

STEPS = 4
HALO = 8


time_step = 0.25


def with_halo(cells, axis, dim, width):
    count = lax.axis_size(axis)
    ends = count - 1
    head = lax.slice_in_dim(cells, 0, width, axis=dim)
    tail = lax.slice_in_dim(cells, cells.shape[dim] - width, cells.shape[dim], axis=dim)
    return jnp.concatenate(
        [
            lax.ppermute(tail, axis, [(i, (i + 1) % count) for i in range(ends)]),
            cells,
            lax.ppermute(head, axis, [((i + 1) % count, i) for i in range(ends)]),
        ],
        axis=dim,
    )


def potential(field):
    return field + 0.25 * jnp.tanh(field)


def advance(field, kappa, along_rows, along_cols):
    wide = jnp.pad(field, ((0, 0), (1, 1), (1, 1)))
    shaped = potential(wide)
    centre = wide[:, 1:-1, 1:-1]
    spread = (
        shaped[:, :-2, 1:-1]
        + shaped[:, 2:, 1:-1]
        + shaped[:, 1:-1, :-2]
        + shaped[:, 1:-1, 2:]
        - 4.0 * shaped[:, 1:-1, 1:-1]
    )
    transport = (
        jnp.maximum(along_rows, 0.0) * (centre - wide[:, :-2, 1:-1])
        + jnp.minimum(along_rows, 0.0) * (wide[:, 2:, 1:-1] - centre)
        + jnp.maximum(along_cols, 0.0) * (centre - wide[:, 1:-1, :-2])
        + jnp.minimum(along_cols, 0.0) * (wide[:, 1:-1, 2:] - centre)
    )
    return centre + time_step * (kappa * spread - transport)


def fine(field, kappa, along_rows, along_cols, inside):
    for step in range(STEPS):
        field = jnp.where(inside, advance(field, kappa, along_rows, along_cols), 0.0)
    return field[:, STEPS:-STEPS]


def pad_cols(x):
    return jnp.pad(x, [(0, 0)] * (x.ndim - 1) + [(HALO, HALO)])


def own_window(x, start, width):
    return lax.dynamic_slice_in_dim(pad_cols(x), start, width, axis=x.ndim - 1)


def scan_kernel(fine_ref, old_ref, pair_ref, begin_ref, ends_ref, adjoint_ref):
    slabs = fine_ref.shape[0]
    width = ends_ref.shape[2]
    begin = begin_ref[...]
    ends = []
    for slab in range(slabs):
        carried = fine_ref[slab] - pair_ref[slab, 0] * old_ref[slab]
        begin = pair_ref[slab, 0] * begin + carried
        ends.append(begin)
        ends_ref[slab] = begin[:, HALO : HALO + width]
    adjoint = ends[slabs - 1] - pair_ref[slabs - 1, 1]
    adjoint_ref[slabs - 1] = adjoint
    for slab in range(slabs - 2, -1, -1):
        adjoint = (ends[slab] - pair_ref[slab, 1]) + pair_ref[slab + 1, 0] * adjoint
        adjoint_ref[slab] = adjoint


def scans(fine_ends, old, pair, begin, width):
    slabs, rows, wide = fine_ends.shape
    tile = 8
    stacked = pl.BlockSpec((slabs, tile, wide), lambda i: (0, i, 0))
    inner = pl.BlockSpec((slabs, tile, width), lambda i: (0, i, 0))
    both = pl.BlockSpec((slabs, 2, tile, wide), lambda i: (0, 0, i, 0))
    single = pl.BlockSpec((tile, wide), lambda i: (i, 0))
    return pl.pallas_call(
        scan_kernel,
        grid=(rows // tile,),
        in_specs=[stacked, stacked, both, single],
        out_specs=[inner, stacked],
        out_shape=[
            jax.ShapeDtypeStruct((slabs, rows, width), fine_ends.dtype),
            jax.ShapeDtypeStruct(fine_ends.shape, fine_ends.dtype),
        ],
    )(fine_ends, old, pair, begin)


def on_device(start_state, old_starts, conductivity, velocity, coarse_gain, targets):
    blocks = lax.axis_size("tm")
    block = lax.axis_index("tm")
    rows, cols = start_state.shape
    width = cols // blocks
    wide = width + 2 * HALO

    def send_windows(x):
        main = x.reshape(rows, blocks, width).transpose(1, 0, 2)
        left = jnp.pad(main[:-1, :, width - HALO :], ((1, 0), (0, 0), (0, 0)))
        right = jnp.pad(main[1:, :, :HALO], ((0, 1), (0, 0), (0, 0)))
        return jnp.concatenate([left, main, right], axis=2)

    def to_blocks(x):
        return lax.all_to_all(send_windows(x), "tm", 0, 0, tiled=True)

    old = to_blocks(old_starts[0])
    pair = lax.all_to_all(
        jnp.stack([send_windows(coarse_gain[0]), send_windows(targets[0])], axis=1),
        "tm", 0, 0, tiled=True,
    )
    old, conductivity, velocity, start_state = lax.optimization_barrier(
        (old, conductivity, velocity, start_state)
    )

    first = block * width
    kappa = own_window(conductivity, first, wide)
    flow = own_window(velocity, first, wide)
    begin = own_window(start_state, first, wide)
    column = first - HALO + lax.broadcasted_iota(jnp.int32, (1, 1, wide), 2)
    strip = lax.axis_index("space")
    row = strip * rows - STEPS + lax.broadcasted_iota(jnp.int32, (1, rows + 2 * STEPS, 1), 1)
    inside = (column >= 0) & (column < cols) & (row >= 0) & (row < rows * lax.axis_size("space"))
    slabs = old.shape[0]
    fields = jnp.concatenate([old, kappa[None], flow], axis=0)
    fields = with_halo(fields, "space", 1, STEPS)
    old_rows = fields[:slabs]
    kappa_rows = fields[slabs]
    flow_rows = fields[slabs + 1 :]

    fine_ends, pullback = jax.vjp(
        lambda k: fine(old_rows, k, flow_rows[0], flow_rows[1], inside), kappa_rows
    )
    interior, adjoint = scans(fine_ends, old, pair, begin, width)
    (grad_rows,) = pullback(adjoint)
    count = lax.axis_size("space")
    ends = count - 1
    from_below = lax.ppermute(grad_rows[:STEPS], "space", [((i + 1) % count, i) for i in range(ends)])
    from_above = lax.ppermute(grad_rows[-STEPS:], "space", [(i, (i + 1) % count) for i in range(ends)])
    grad_window = grad_rows[STEPS:-STEPS]
    grad_window = grad_window.at[-STEPS:].add(from_below).at[:STEPS].add(from_above)

    new_end = lax.all_to_all(interior, "tm", 0, 2, tiled=True)
    own = grad_window[:, HALO : HALO + width]
    copies = jnp.broadcast_to(own[None], (blocks,) + own.shape)
    gradient = lax.all_to_all(copies, "tm", 0, 2, tiled=True)[0]
    return (new_end, gradient)


def solution(mesh):
    in_specs = (
        P("space", None),
        P("tm", "space", None),
        P("space", None),
        P(None, "space", None),
        P("tm", "space", None),
        P("tm", "space", None),
    )
    out_specs = (P("tm", "space", None), P("space", None))
    return jax.shard_map(
        on_device, mesh=mesh, in_specs=in_specs, out_specs=out_specs, check_vma=False
    )
```

```python
import jax
import jax.numpy as jnp
from jax import lax
from jax.experimental import pallas as pl
from jax.sharding import PartitionSpec as P

STEPS = 4
HALO = 8


time_step = 0.25


def with_halo(cells, axis, dim, width):
    count = lax.axis_size(axis)
    ends = count - 1
    head = lax.slice_in_dim(cells, 0, width, axis=dim)
    tail = lax.slice_in_dim(cells, cells.shape[dim] - width, cells.shape[dim], axis=dim)
    return jnp.concatenate(
        [
            lax.ppermute(tail, axis, [(i, (i + 1) % count) for i in range(ends)]),
            cells,
            lax.ppermute(head, axis, [((i + 1) % count, i) for i in range(ends)]),
        ],
        axis=dim,
    )


def potential(field):
    return field + 0.25 * jnp.tanh(field)


def advance(field, kappa, along_rows, along_cols):
    wide = jnp.pad(field, ((0, 0), (1, 1), (1, 1)))
    shaped = potential(wide)
    centre = wide[:, 1:-1, 1:-1]
    spread = (
        shaped[:, :-2, 1:-1]
        + shaped[:, 2:, 1:-1]
        + shaped[:, 1:-1, :-2]
        + shaped[:, 1:-1, 2:]
        - 4.0 * shaped[:, 1:-1, 1:-1]
    )
    transport = (
        jnp.maximum(along_rows, 0.0) * (centre - wide[:, :-2, 1:-1])
        + jnp.minimum(along_rows, 0.0) * (wide[:, 2:, 1:-1] - centre)
        + jnp.maximum(along_cols, 0.0) * (centre - wide[:, 1:-1, :-2])
        + jnp.minimum(along_cols, 0.0) * (wide[:, 1:-1, 2:] - centre)
    )
    return centre + time_step * (kappa * spread - transport)


def fine(field, kappa, along_rows, along_cols, inside):
    for step in range(STEPS):
        field = jnp.where(inside, advance(field, kappa, along_rows, along_cols), 0.0)
    return field[:, STEPS:-STEPS]


def pad_cols(x):
    return jnp.pad(x, [(0, 0)] * (x.ndim - 1) + [(HALO, HALO)])


def own_window(x, start, width):
    return lax.dynamic_slice_in_dim(pad_cols(x), start, width, axis=x.ndim - 1)


def scan_kernel(fine_ref, old_ref, pair_ref, begin_ref, ends_ref, adjoint_ref):
    slabs = fine_ref.shape[0]
    width = ends_ref.shape[2]
    begin = begin_ref[...]
    ends = []
    for slab in range(slabs):
        carried = fine_ref[slab] - pair_ref[slab, 0] * old_ref[slab]
        begin = pair_ref[slab, 0] * begin + carried
        ends.append(begin)
        ends_ref[slab] = begin[:, HALO : HALO + width]
    adjoint = ends[slabs - 1] - pair_ref[slabs - 1, 1]
    adjoint_ref[slabs - 1] = adjoint
    for slab in range(slabs - 2, -1, -1):
        adjoint = (ends[slab] - pair_ref[slab, 1]) + pair_ref[slab + 1, 0] * adjoint
        adjoint_ref[slab] = adjoint


def scans(fine_ends, old, pair, begin, width):
    slabs, rows, wide = fine_ends.shape
    tile = 8
    stacked = pl.BlockSpec((slabs, tile, wide), lambda i: (0, i, 0))
    inner = pl.BlockSpec((slabs, tile, width), lambda i: (0, i, 0))
    both = pl.BlockSpec((slabs, 2, tile, wide), lambda i: (0, 0, i, 0))
    single = pl.BlockSpec((tile, wide), lambda i: (i, 0))
    return pl.pallas_call(
        scan_kernel,
        grid=(rows // tile,),
        in_specs=[stacked, stacked, both, single],
        out_specs=[inner, stacked],
        out_shape=[
            jax.ShapeDtypeStruct((slabs, rows, width), fine_ends.dtype),
            jax.ShapeDtypeStruct(fine_ends.shape, fine_ends.dtype),
        ],
    )(fine_ends, old, pair, begin)


def on_device(start_state, old_starts, conductivity, velocity, coarse_gain, targets):
    blocks = lax.axis_size("tm")
    block = lax.axis_index("tm")
    rows, cols = start_state.shape
    width = cols // blocks
    wide = width + 2 * HALO

    def send_windows(x):
        main = x.reshape(rows, blocks, width).transpose(1, 0, 2)
        left = jnp.pad(main[:-1, :, width - HALO :], ((1, 0), (0, 0), (0, 0)))
        right = jnp.pad(main[1:, :, :HALO], ((0, 1), (0, 0), (0, 0)))
        return jnp.concatenate([left, main, right], axis=2)

    def to_blocks(x):
        return lax.all_to_all(send_windows(x), "tm", 0, 0, tiled=True)

    old = to_blocks(old_starts[0])
    pair = jnp.stack([send_windows(coarse_gain[0]), send_windows(targets[0])], axis=1)
    old, conductivity, velocity, start_state = lax.optimization_barrier(
        (old, conductivity, velocity, start_state)
    )

    first = block * width
    kappa = own_window(conductivity, first, wide)
    flow = own_window(velocity, first, wide)
    begin = own_window(start_state, first, wide)
    column = first - HALO + lax.broadcasted_iota(jnp.int32, (1, 1, wide), 2)
    strip = lax.axis_index("space")
    row = strip * rows - STEPS + lax.broadcasted_iota(jnp.int32, (1, rows + 2 * STEPS, 1), 1)
    inside = (column >= 0) & (column < cols) & (row >= 0) & (row < rows * lax.axis_size("space"))
    slabs = old.shape[0]
    fields = jnp.concatenate([old, kappa[None], flow], axis=0)
    fields = with_halo(fields, "space", 1, STEPS)
    fields, pair = lax.optimization_barrier((fields, pair))
    pair = lax.all_to_all(pair, "tm", 0, 0, tiled=True)
    old_rows = fields[:slabs]
    kappa_rows = fields[slabs]
    flow_rows = fields[slabs + 1 :]

    fine_ends, pullback = jax.vjp(
        lambda k: fine(old_rows, k, flow_rows[0], flow_rows[1], inside), kappa_rows
    )
    interior, adjoint = scans(fine_ends, old, pair, begin, width)
    (grad_rows,) = pullback(adjoint)
    count = lax.axis_size("space")
    ends = count - 1
    from_below = lax.ppermute(grad_rows[:STEPS], "space", [((i + 1) % count, i) for i in range(ends)])
    from_above = lax.ppermute(grad_rows[-STEPS:], "space", [(i, (i + 1) % count) for i in range(ends)])
    grad_window = grad_rows[STEPS:-STEPS]
    grad_window = grad_window.at[-STEPS:].add(from_below).at[:STEPS].add(from_above)

    new_end = lax.all_to_all(interior, "tm", 0, 2, tiled=True)
    own = grad_window[:, HALO : HALO + width]
    copies = jnp.broadcast_to(own[None], (blocks,) + own.shape)
    gradient = lax.all_to_all(copies, "tm", 0, 2, tiled=True)[0]
    return (new_end, gradient)


def solution(mesh):
    in_specs = (
        P("space", None),
        P("tm", "space", None),
        P("space", None),
        P(None, "space", None),
        P("tm", "space", None),
        P("tm", "space", None),
    )
    out_specs = (P("tm", "space", None), P("space", None))
    return jax.shard_map(
        on_device, mesh=mesh, in_specs=in_specs, out_specs=out_specs, check_vma=False
    )
```

```python
import jax
import jax.numpy as jnp
from jax import lax
from jax.experimental import pallas as pl
from jax.sharding import PartitionSpec as P

STEPS = 4
HALO = 8


time_step = 0.25


def with_halo(cells, axis, dim, width):
    count = lax.axis_size(axis)
    ends = count - 1
    head = lax.slice_in_dim(cells, 0, width, axis=dim)
    tail = lax.slice_in_dim(cells, cells.shape[dim] - width, cells.shape[dim], axis=dim)
    return jnp.concatenate(
        [
            lax.ppermute(tail, axis, [(i, (i + 1) % count) for i in range(ends)]),
            cells,
            lax.ppermute(head, axis, [((i + 1) % count, i) for i in range(ends)]),
        ],
        axis=dim,
    )


def potential(field):
    return field + 0.25 * jnp.tanh(field)


def advance(field, kappa, along_rows, along_cols):
    wide = jnp.pad(field, ((0, 0), (1, 1), (1, 1)))
    shaped = potential(wide)
    centre = wide[:, 1:-1, 1:-1]
    spread = (
        shaped[:, :-2, 1:-1]
        + shaped[:, 2:, 1:-1]
        + shaped[:, 1:-1, :-2]
        + shaped[:, 1:-1, 2:]
        - 4.0 * shaped[:, 1:-1, 1:-1]
    )
    transport = (
        jnp.maximum(along_rows, 0.0) * (centre - wide[:, :-2, 1:-1])
        + jnp.minimum(along_rows, 0.0) * (wide[:, 2:, 1:-1] - centre)
        + jnp.maximum(along_cols, 0.0) * (centre - wide[:, 1:-1, :-2])
        + jnp.minimum(along_cols, 0.0) * (wide[:, 1:-1, 2:] - centre)
    )
    return centre + time_step * (kappa * spread - transport)


def fine(field, kappa, along_rows, along_cols, inside):
    for step in range(STEPS):
        field = jnp.where(inside, advance(field, kappa, along_rows, along_cols), 0.0)
    return field[:, STEPS:-STEPS]


def pad_cols(x):
    return jnp.pad(x, [(0, 0)] * (x.ndim - 1) + [(HALO, HALO)])


def own_window(x, start, width):
    return lax.dynamic_slice_in_dim(pad_cols(x), start, width, axis=x.ndim - 1)


def scan_kernel(fine_ref, old_ref, pair_ref, begin_ref, ends_ref, adjoint_ref):
    slabs = fine_ref.shape[0]
    width = ends_ref.shape[2]
    begin = begin_ref[...]
    ends = []
    for slab in range(slabs):
        carried = fine_ref[slab] - pair_ref[slab, 0] * old_ref[slab]
        begin = pair_ref[slab, 0] * begin + carried
        ends.append(begin)
        ends_ref[slab] = begin[:, HALO : HALO + width]
    adjoint = ends[slabs - 1] - pair_ref[slabs - 1, 1]
    adjoint_ref[slabs - 1] = adjoint
    for slab in range(slabs - 2, -1, -1):
        adjoint = (ends[slab] - pair_ref[slab, 1]) + pair_ref[slab + 1, 0] * adjoint
        adjoint_ref[slab] = adjoint


def scans(fine_ends, old, pair, begin, width):
    slabs, rows, wide = fine_ends.shape
    tile = 8
    stacked = pl.BlockSpec((slabs, tile, wide), lambda i: (0, i, 0))
    inner = pl.BlockSpec((slabs, tile, width), lambda i: (0, i, 0))
    both = pl.BlockSpec((slabs, 2, tile, wide), lambda i: (0, 0, i, 0))
    single = pl.BlockSpec((tile, wide), lambda i: (i, 0))
    return pl.pallas_call(
        scan_kernel,
        grid=(rows // tile,),
        in_specs=[stacked, stacked, both, single],
        out_specs=[inner, stacked],
        out_shape=[
            jax.ShapeDtypeStruct((slabs, rows, width), fine_ends.dtype),
            jax.ShapeDtypeStruct(fine_ends.shape, fine_ends.dtype),
        ],
    )(fine_ends, old, pair, begin)


def on_device(start_state, old_starts, conductivity, velocity, coarse_gain, targets):
    blocks = lax.axis_size("tm")
    block = lax.axis_index("tm")
    rows, cols = start_state.shape
    width = cols // blocks
    wide = width + 2 * HALO

    def send_windows(x):
        main = x.reshape(rows, blocks, width).transpose(1, 0, 2)
        left = jnp.pad(main[:-1, :, width - HALO :], ((1, 0), (0, 0), (0, 0)))
        right = jnp.pad(main[1:, :, :HALO], ((0, 1), (0, 0), (0, 0)))
        return jnp.concatenate([left, main, right], axis=2)

    def to_blocks(x):
        return lax.all_to_all(send_windows(x), "tm", 0, 0, tiled=True)

    old = to_blocks(old_starts[0])
    pair = jnp.stack([send_windows(coarse_gain[0]), send_windows(targets[0])], axis=1)
    old, conductivity, velocity, start_state = lax.optimization_barrier(
        (old, conductivity, velocity, start_state)
    )

    first = block * width
    kappa = own_window(conductivity, first, wide)
    flow = own_window(velocity, first, wide)
    begin = own_window(start_state, first, wide)
    column = first - HALO + lax.broadcasted_iota(jnp.int32, (1, 1, wide), 2)
    strip = lax.axis_index("space")
    row = strip * rows - STEPS + lax.broadcasted_iota(jnp.int32, (1, rows + 2 * STEPS, 1), 1)
    inside = (column >= 0) & (column < cols) & (row >= 0) & (row < rows * lax.axis_size("space"))
    slabs = old.shape[0]
    fields = jnp.concatenate([old, kappa[None], flow], axis=0)
    fields = with_halo(fields, "space", 1, STEPS)
    fields, pair = lax.optimization_barrier((fields, pair))
    pair = lax.all_to_all(pair, "tm", 0, 0, tiled=True)
    old_rows = fields[:slabs]
    kappa_rows = fields[slabs]
    flow_rows = fields[slabs + 1 :]

    fine_ends, pullback = jax.vjp(
        lambda k: fine(old_rows, k, flow_rows[0], flow_rows[1], inside), kappa_rows
    )
    interior, adjoint = scans(fine_ends, old, pair, begin, width)
    (grad_rows,) = pullback(adjoint)
    new_end = lax.all_to_all(interior, "tm", 0, 2, tiled=True)
    new_end, grad_rows = lax.optimization_barrier((new_end, grad_rows))
    count = lax.axis_size("space")
    ends = count - 1
    from_below = lax.ppermute(grad_rows[:STEPS], "space", [((i + 1) % count, i) for i in range(ends)])
    from_above = lax.ppermute(grad_rows[-STEPS:], "space", [(i, (i + 1) % count) for i in range(ends)])
    grad_window = grad_rows[STEPS:-STEPS]
    grad_window = grad_window.at[-STEPS:].add(from_below).at[:STEPS].add(from_above)

    own = grad_window[:, HALO : HALO + width]
    copies = jnp.broadcast_to(own[None], (blocks,) + own.shape)
    gradient = lax.all_to_all(copies, "tm", 0, 2, tiled=True)[0]
    return (new_end, gradient)


def solution(mesh):
    in_specs = (
        P("space", None),
        P("tm", "space", None),
        P("space", None),
        P(None, "space", None),
        P("tm", "space", None),
        P("tm", "space", None),
    )
    out_specs = (P("tm", "space", None), P("space", None))
    return jax.shard_map(
        on_device, mesh=mesh, in_specs=in_specs, out_specs=out_specs, check_vma=False
    )
```

```python
import jax
import jax.numpy as jnp
from jax import lax
from jax.experimental import pallas as pl
from jax.sharding import PartitionSpec as P

STEPS = 4
HALO = 8


time_step = 0.25


def with_halo(cells, axis, dim, width):
    count = lax.axis_size(axis)
    ends = count - 1
    head = lax.slice_in_dim(cells, 0, width, axis=dim)
    tail = lax.slice_in_dim(cells, cells.shape[dim] - width, cells.shape[dim], axis=dim)
    return jnp.concatenate(
        [
            lax.ppermute(tail, axis, [(i, (i + 1) % count) for i in range(ends)]),
            cells,
            lax.ppermute(head, axis, [((i + 1) % count, i) for i in range(ends)]),
        ],
        axis=dim,
    )


def potential(field):
    return field + 0.25 * jnp.tanh(field)


def advance(field, kappa, along_rows, along_cols):
    wide = jnp.pad(field, ((0, 0), (1, 1), (1, 1)))
    shaped = potential(wide)
    centre = wide[:, 1:-1, 1:-1]
    spread = (
        shaped[:, :-2, 1:-1]
        + shaped[:, 2:, 1:-1]
        + shaped[:, 1:-1, :-2]
        + shaped[:, 1:-1, 2:]
        - 4.0 * shaped[:, 1:-1, 1:-1]
    )
    transport = (
        jnp.maximum(along_rows, 0.0) * (centre - wide[:, :-2, 1:-1])
        + jnp.minimum(along_rows, 0.0) * (wide[:, 2:, 1:-1] - centre)
        + jnp.maximum(along_cols, 0.0) * (centre - wide[:, 1:-1, :-2])
        + jnp.minimum(along_cols, 0.0) * (wide[:, 1:-1, 2:] - centre)
    )
    return centre + time_step * (kappa * spread - transport)


def fine(field, kappa, along_rows, along_cols, inside):
    for step in range(STEPS):
        field = jnp.where(inside, advance(field, kappa, along_rows, along_cols), 0.0)
    return field[:, STEPS:-STEPS]


def pad_cols(x):
    return jnp.pad(x, [(0, 0)] * (x.ndim - 1) + [(HALO, HALO)])


def own_window(x, start, width):
    return lax.dynamic_slice_in_dim(pad_cols(x), start, width, axis=x.ndim - 1)


def scan_kernel(fine_ref, old_ref, gain_ref, target_ref, begin_ref, ends_ref, adjoint_ref):
    slabs = fine_ref.shape[0]
    width = ends_ref.shape[2]
    begin = begin_ref[...]
    ends = []
    for slab in range(slabs):
        carried = fine_ref[slab] - gain_ref[slab] * old_ref[slab]
        begin = gain_ref[slab] * begin + carried
        ends.append(begin)
        ends_ref[slab] = begin[:, HALO : HALO + width]
    adjoint = ends[slabs - 1] - target_ref[slabs - 1]
    adjoint_ref[slabs - 1] = adjoint
    for slab in range(slabs - 2, -1, -1):
        adjoint = (ends[slab] - target_ref[slab]) + gain_ref[slab + 1] * adjoint
        adjoint_ref[slab] = adjoint


def scans(fine_ends, old, gain, target, begin, width):
    slabs, rows, wide = fine_ends.shape
    tile = 8
    stacked = pl.BlockSpec((slabs, tile, wide), lambda i: (0, i, 0))
    inner = pl.BlockSpec((slabs, tile, width), lambda i: (0, i, 0))
    single = pl.BlockSpec((tile, wide), lambda i: (i, 0))
    return pl.pallas_call(
        scan_kernel,
        grid=(rows // tile,),
        in_specs=[stacked, stacked, stacked, stacked, single],
        out_specs=[inner, stacked],
        out_shape=[
            jax.ShapeDtypeStruct((slabs, rows, width), fine_ends.dtype),
            jax.ShapeDtypeStruct(fine_ends.shape, fine_ends.dtype),
        ],
    )(fine_ends, old, gain, target, begin)


def on_device(start_state, old_starts, conductivity, velocity, coarse_gain, targets):
    blocks = lax.axis_size("tm")
    block = lax.axis_index("tm")
    rows, cols = start_state.shape
    width = cols // blocks
    wide = width + 2 * HALO

    def send_windows(x):
        main = x.reshape(rows, blocks, width).transpose(1, 0, 2)
        left = jnp.pad(main[:-1, :, width - HALO :], ((1, 0), (0, 0), (0, 0)))
        right = jnp.pad(main[1:, :, :HALO], ((0, 1), (0, 0), (0, 0)))
        return jnp.concatenate([left, main, right], axis=2)

    def to_blocks(x):
        return lax.all_to_all(send_windows(x), "tm", 0, 0, tiled=True)

    old = to_blocks(old_starts[0])
    target_out = send_windows(targets[0])
    pieces = [lax.dynamic_index_in_dim(target_out, block, 0, keepdims=False)]
    for shift in range(1, blocks):
        piece = lax.dynamic_index_in_dim(target_out, (block + shift) % blocks, 0, keepdims=False)
        pieces.append(lax.ppermute(piece, "tm", [(i, (i + shift) % blocks) for i in range(blocks)]))
    target = jnp.take(jnp.stack(pieces), (block - jnp.arange(blocks)) % blocks, axis=0)
    gain_out = send_windows(coarse_gain[0])
    old, conductivity, velocity, start_state = lax.optimization_barrier(
        (old, conductivity, velocity, start_state)
    )

    first = block * width
    kappa = own_window(conductivity, first, wide)
    flow = own_window(velocity, first, wide)
    begin = own_window(start_state, first, wide)
    column = first - HALO + lax.broadcasted_iota(jnp.int32, (1, 1, wide), 2)
    strip = lax.axis_index("space")
    row = strip * rows - STEPS + lax.broadcasted_iota(jnp.int32, (1, rows + 2 * STEPS, 1), 1)
    inside = (column >= 0) & (column < cols) & (row >= 0) & (row < rows * lax.axis_size("space"))
    slabs = old.shape[0]
    fields = jnp.concatenate([old, kappa[None], flow], axis=0)
    fields = with_halo(fields, "space", 1, STEPS)
    fields, gain_out = lax.optimization_barrier((fields, gain_out))
    gain = lax.all_to_all(gain_out, "tm", 0, 0, tiled=True)
    old_rows = fields[:slabs]
    kappa_rows = fields[slabs]
    flow_rows = fields[slabs + 1 :]

    fine_ends, pullback = jax.vjp(
        lambda k: fine(old_rows, k, flow_rows[0], flow_rows[1], inside), kappa_rows
    )
    interior, adjoint = scans(fine_ends, old, gain, target, begin, width)
    (grad_rows,) = pullback(adjoint)
    count = lax.axis_size("space")
    ends = count - 1
    from_below = lax.ppermute(grad_rows[:STEPS], "space", [((i + 1) % count, i) for i in range(ends)])
    from_above = lax.ppermute(grad_rows[-STEPS:], "space", [(i, (i + 1) % count) for i in range(ends)])
    grad_window = grad_rows[STEPS:-STEPS]
    grad_window = grad_window.at[-STEPS:].add(from_below).at[:STEPS].add(from_above)

    new_end = lax.all_to_all(interior, "tm", 0, 2, tiled=True)
    own = grad_window[:, HALO : HALO + width]
    copies = jnp.broadcast_to(own[None], (blocks,) + own.shape)
    gradient = lax.all_to_all(copies, "tm", 0, 2, tiled=True)[0]
    return (new_end, gradient)


def solution(mesh):
    in_specs = (
        P("space", None),
        P("tm", "space", None),
        P("space", None),
        P(None, "space", None),
        P("tm", "space", None),
        P("tm", "space", None),
    )
    out_specs = (P("tm", "space", None), P("space", None))
    return jax.shard_map(
        on_device, mesh=mesh, in_specs=in_specs, out_specs=out_specs, check_vma=False
    )
```

```python
import jax
import jax.numpy as jnp
from jax import lax
from jax.experimental import pallas as pl
from jax.sharding import PartitionSpec as P

STEPS = 4
HALO = 8


time_step = 0.25


def with_halo(cells, axis, dim, width):
    count = lax.axis_size(axis)
    ends = count - 1
    head = lax.slice_in_dim(cells, 0, width, axis=dim)
    tail = lax.slice_in_dim(cells, cells.shape[dim] - width, cells.shape[dim], axis=dim)
    return jnp.concatenate(
        [
            lax.ppermute(tail, axis, [(i, (i + 1) % count) for i in range(ends)]),
            cells,
            lax.ppermute(head, axis, [((i + 1) % count, i) for i in range(ends)]),
        ],
        axis=dim,
    )


def potential(field):
    return field + 0.25 * jnp.tanh(field)


def advance(field, kappa, along_rows, along_cols):
    wide = jnp.pad(field, ((0, 0), (1, 1), (1, 1)))
    shaped = potential(wide)
    centre = wide[:, 1:-1, 1:-1]
    spread = (
        shaped[:, :-2, 1:-1]
        + shaped[:, 2:, 1:-1]
        + shaped[:, 1:-1, :-2]
        + shaped[:, 1:-1, 2:]
        - 4.0 * shaped[:, 1:-1, 1:-1]
    )
    transport = (
        jnp.maximum(along_rows, 0.0) * (centre - wide[:, :-2, 1:-1])
        + jnp.minimum(along_rows, 0.0) * (wide[:, 2:, 1:-1] - centre)
        + jnp.maximum(along_cols, 0.0) * (centre - wide[:, 1:-1, :-2])
        + jnp.minimum(along_cols, 0.0) * (wide[:, 1:-1, 2:] - centre)
    )
    return centre + time_step * (kappa * spread - transport)


def fine(field, kappa, along_rows, along_cols, inside):
    for step in range(STEPS):
        field = jnp.where(inside, advance(field, kappa, along_rows, along_cols), 0.0)
    return field[:, STEPS:-STEPS]


def pad_cols(x):
    return jnp.pad(x, [(0, 0)] * (x.ndim - 1) + [(HALO, HALO)])


def own_window(x, start, width):
    return lax.dynamic_slice_in_dim(pad_cols(x), start, width, axis=x.ndim - 1)


def scan_kernel(fine_ref, old_ref, pair_ref, begin_ref, ends_ref, adjoint_ref):
    slabs = fine_ref.shape[0]
    width = ends_ref.shape[2]
    begin = begin_ref[...]
    ends = []
    for slab in range(slabs):
        carried = fine_ref[slab] - pair_ref[slab, 0] * old_ref[slab]
        begin = pair_ref[slab, 0] * begin + carried
        ends.append(begin)
        ends_ref[slab] = begin[:, HALO : HALO + width]
    adjoint = ends[slabs - 1] - pair_ref[slabs - 1, 1]
    adjoint_ref[slabs - 1] = adjoint
    for slab in range(slabs - 2, -1, -1):
        adjoint = (ends[slab] - pair_ref[slab, 1]) + pair_ref[slab + 1, 0] * adjoint
        adjoint_ref[slab] = adjoint


def scans(fine_ends, old, pair, begin, width):
    slabs, rows, wide = fine_ends.shape
    tile = 16
    stacked = pl.BlockSpec((slabs, tile, wide), lambda i: (0, i, 0))
    inner = pl.BlockSpec((slabs, tile, width), lambda i: (0, i, 0))
    both = pl.BlockSpec((slabs, 2, tile, wide), lambda i: (0, 0, i, 0))
    single = pl.BlockSpec((tile, wide), lambda i: (i, 0))
    return pl.pallas_call(
        scan_kernel,
        grid=(rows // tile,),
        in_specs=[stacked, stacked, both, single],
        out_specs=[inner, stacked],
        out_shape=[
            jax.ShapeDtypeStruct((slabs, rows, width), fine_ends.dtype),
            jax.ShapeDtypeStruct(fine_ends.shape, fine_ends.dtype),
        ],
    )(fine_ends, old, pair, begin)


def on_device(start_state, old_starts, conductivity, velocity, coarse_gain, targets):
    blocks = lax.axis_size("tm")
    block = lax.axis_index("tm")
    rows, cols = start_state.shape
    width = cols // blocks
    wide = width + 2 * HALO

    def send_windows(x):
        main = x.reshape(rows, blocks, width).transpose(1, 0, 2)
        left = jnp.pad(main[:-1, :, width - HALO :], ((1, 0), (0, 0), (0, 0)))
        right = jnp.pad(main[1:, :, :HALO], ((0, 1), (0, 0), (0, 0)))
        return jnp.concatenate([left, main, right], axis=2)

    def to_blocks(x):
        return lax.all_to_all(send_windows(x), "tm", 0, 0, tiled=True)

    old = to_blocks(old_starts[0])
    pair = jnp.stack([send_windows(coarse_gain[0]), send_windows(targets[0])], axis=1)
    old, conductivity, velocity, start_state = lax.optimization_barrier(
        (old, conductivity, velocity, start_state)
    )

    first = block * width
    kappa = own_window(conductivity, first, wide)
    flow = own_window(velocity, first, wide)
    begin = own_window(start_state, first, wide)
    column = first - HALO + lax.broadcasted_iota(jnp.int32, (1, 1, wide), 2)
    strip = lax.axis_index("space")
    row = strip * rows - STEPS + lax.broadcasted_iota(jnp.int32, (1, rows + 2 * STEPS, 1), 1)
    inside = (column >= 0) & (column < cols) & (row >= 0) & (row < rows * lax.axis_size("space"))
    slabs = old.shape[0]
    fields = jnp.concatenate([old, kappa[None], flow], axis=0)
    fields = with_halo(fields, "space", 1, STEPS)
    fields, pair = lax.optimization_barrier((fields, pair))
    pair = lax.all_to_all(pair, "tm", 0, 0, tiled=True)
    old_rows = fields[:slabs]
    kappa_rows = fields[slabs]
    flow_rows = fields[slabs + 1 :]

    fine_ends, pullback = jax.vjp(
        lambda k: fine(old_rows, k, flow_rows[0], flow_rows[1], inside), kappa_rows
    )
    interior, adjoint = scans(fine_ends, old, pair, begin, width)
    (grad_rows,) = pullback(adjoint)
    count = lax.axis_size("space")
    ends = count - 1
    from_below = lax.ppermute(grad_rows[:STEPS], "space", [((i + 1) % count, i) for i in range(ends)])
    from_above = lax.ppermute(grad_rows[-STEPS:], "space", [(i, (i + 1) % count) for i in range(ends)])
    grad_window = grad_rows[STEPS:-STEPS]
    grad_window = grad_window.at[-STEPS:].add(from_below).at[:STEPS].add(from_above)

    new_end = lax.all_to_all(interior, "tm", 0, 2, tiled=True)
    own = grad_window[:, HALO : HALO + width]
    copies = jnp.broadcast_to(own[None], (blocks,) + own.shape)
    gradient = lax.all_to_all(copies, "tm", 0, 2, tiled=True)[0]
    return (new_end, gradient)


def solution(mesh):
    in_specs = (
        P("space", None),
        P("tm", "space", None),
        P("space", None),
        P(None, "space", None),
        P("tm", "space", None),
        P("tm", "space", None),
    )
    out_specs = (P("tm", "space", None), P("space", None))
    return jax.shard_map(
        on_device, mesh=mesh, in_specs=in_specs, out_specs=out_specs, check_vma=False
    )
```

```python
import jax
import jax.numpy as jnp
from jax import lax
from jax.experimental import pallas as pl
from jax.sharding import PartitionSpec as P

STEPS = 4
HALO = 8


time_step = 0.25


def with_halo(cells, axis, dim, width):
    count = lax.axis_size(axis)
    ends = count - 1
    head = lax.slice_in_dim(cells, 0, width, axis=dim)
    tail = lax.slice_in_dim(cells, cells.shape[dim] - width, cells.shape[dim], axis=dim)
    return jnp.concatenate(
        [
            lax.ppermute(tail, axis, [(i, (i + 1) % count) for i in range(ends)]),
            cells,
            lax.ppermute(head, axis, [((i + 1) % count, i) for i in range(ends)]),
        ],
        axis=dim,
    )


def potential(field):
    return field + 0.25 * jnp.tanh(field)


def advance(field, kappa, along_rows, along_cols):
    wide = jnp.pad(field, ((0, 0), (1, 1), (1, 1)))
    shaped = potential(wide)
    centre = wide[:, 1:-1, 1:-1]
    spread = (
        shaped[:, :-2, 1:-1]
        + shaped[:, 2:, 1:-1]
        + shaped[:, 1:-1, :-2]
        + shaped[:, 1:-1, 2:]
        - 4.0 * shaped[:, 1:-1, 1:-1]
    )
    transport = (
        jnp.maximum(along_rows, 0.0) * (centre - wide[:, :-2, 1:-1])
        + jnp.minimum(along_rows, 0.0) * (wide[:, 2:, 1:-1] - centre)
        + jnp.maximum(along_cols, 0.0) * (centre - wide[:, 1:-1, :-2])
        + jnp.minimum(along_cols, 0.0) * (wide[:, 1:-1, 2:] - centre)
    )
    return centre + time_step * (kappa * spread - transport)


def fine(field, kappa, along_rows, along_cols, inside):
    for step in range(STEPS):
        field = jnp.where(inside, advance(field, kappa, along_rows, along_cols), 0.0)
    return field[:, STEPS:-STEPS]


def pad_cols(x):
    return jnp.pad(x, [(0, 0)] * (x.ndim - 1) + [(HALO, HALO)])


def own_window(x, start, width):
    return lax.dynamic_slice_in_dim(pad_cols(x), start, width, axis=x.ndim - 1)


def scan_kernel(fine_ref, old_ref, pair_ref, begin_ref, ends_ref, adjoint_ref):
    slabs = fine_ref.shape[0]
    width = ends_ref.shape[2]
    begin = begin_ref[...]
    ends = []
    for slab in range(slabs):
        carried = fine_ref[slab] - pair_ref[slab, 0] * old_ref[slab]
        begin = pair_ref[slab, 0] * begin + carried
        ends.append(begin)
        ends_ref[slab] = begin[:, HALO : HALO + width]
    adjoint = ends[slabs - 1] - pair_ref[slabs - 1, 1]
    adjoint_ref[slabs - 1] = adjoint
    for slab in range(slabs - 2, -1, -1):
        adjoint = (ends[slab] - pair_ref[slab, 1]) + pair_ref[slab + 1, 0] * adjoint
        adjoint_ref[slab] = adjoint


def scans(fine_ends, old, pair, begin, width):
    slabs, rows, wide = fine_ends.shape
    tile = 32
    stacked = pl.BlockSpec((slabs, tile, wide), lambda i: (0, i, 0))
    inner = pl.BlockSpec((slabs, tile, width), lambda i: (0, i, 0))
    both = pl.BlockSpec((slabs, 2, tile, wide), lambda i: (0, 0, i, 0))
    single = pl.BlockSpec((tile, wide), lambda i: (i, 0))
    return pl.pallas_call(
        scan_kernel,
        grid=(rows // tile,),
        in_specs=[stacked, stacked, both, single],
        out_specs=[inner, stacked],
        out_shape=[
            jax.ShapeDtypeStruct((slabs, rows, width), fine_ends.dtype),
            jax.ShapeDtypeStruct(fine_ends.shape, fine_ends.dtype),
        ],
    )(fine_ends, old, pair, begin)


def on_device(start_state, old_starts, conductivity, velocity, coarse_gain, targets):
    blocks = lax.axis_size("tm")
    block = lax.axis_index("tm")
    rows, cols = start_state.shape
    width = cols // blocks
    wide = width + 2 * HALO

    def send_windows(x):
        main = x.reshape(rows, blocks, width).transpose(1, 0, 2)
        left = jnp.pad(main[:-1, :, width - HALO :], ((1, 0), (0, 0), (0, 0)))
        right = jnp.pad(main[1:, :, :HALO], ((0, 1), (0, 0), (0, 0)))
        return jnp.concatenate([left, main, right], axis=2)

    def to_blocks(x):
        return lax.all_to_all(send_windows(x), "tm", 0, 0, tiled=True)

    old = to_blocks(old_starts[0])
    pair = jnp.stack([send_windows(coarse_gain[0]), send_windows(targets[0])], axis=1)
    old, conductivity, velocity, start_state = lax.optimization_barrier(
        (old, conductivity, velocity, start_state)
    )

    first = block * width
    kappa = own_window(conductivity, first, wide)
    flow = own_window(velocity, first, wide)
    begin = own_window(start_state, first, wide)
    column = first - HALO + lax.broadcasted_iota(jnp.int32, (1, 1, wide), 2)
    strip = lax.axis_index("space")
    row = strip * rows - STEPS + lax.broadcasted_iota(jnp.int32, (1, rows + 2 * STEPS, 1), 1)
    inside = (column >= 0) & (column < cols) & (row >= 0) & (row < rows * lax.axis_size("space"))
    slabs = old.shape[0]
    fields = jnp.concatenate([old, kappa[None], flow], axis=0)
    fields = with_halo(fields, "space", 1, STEPS)
    fields, pair = lax.optimization_barrier((fields, pair))
    pair = lax.all_to_all(pair, "tm", 0, 0, tiled=True)
    old_rows = fields[:slabs]
    kappa_rows = fields[slabs]
    flow_rows = fields[slabs + 1 :]

    fine_ends, pullback = jax.vjp(
        lambda k: fine(old_rows, k, flow_rows[0], flow_rows[1], inside), kappa_rows
    )
    interior, adjoint = scans(fine_ends, old, pair, begin, width)
    (grad_rows,) = pullback(adjoint)
    count = lax.axis_size("space")
    ends = count - 1
    from_below = lax.ppermute(grad_rows[:STEPS], "space", [((i + 1) % count, i) for i in range(ends)])
    from_above = lax.ppermute(grad_rows[-STEPS:], "space", [(i, (i + 1) % count) for i in range(ends)])
    grad_window = grad_rows[STEPS:-STEPS]
    grad_window = grad_window.at[-STEPS:].add(from_below).at[:STEPS].add(from_above)

    new_end = lax.all_to_all(interior, "tm", 0, 2, tiled=True)
    own = grad_window[:, HALO : HALO + width]
    copies = jnp.broadcast_to(own[None], (blocks,) + own.shape)
    gradient = lax.all_to_all(copies, "tm", 0, 2, tiled=True)[0]
    return (new_end, gradient)


def solution(mesh):
    in_specs = (
        P("space", None),
        P("tm", "space", None),
        P("space", None),
        P(None, "space", None),
        P("tm", "space", None),
        P("tm", "space", None),
    )
    out_specs = (P("tm", "space", None), P("space", None))
    return jax.shard_map(
        on_device, mesh=mesh, in_specs=in_specs, out_specs=out_specs, check_vma=False
    )
```
